256 devices in a mesh: occ: 32 (over z, y), va: 2 (over x_hi), vb: 4 (over x_lo, core).
Axes of the slice: x: 4 (x_hi: 2, x_lo: 2; x = x_hi * 2 + x_lo), y: 4, z: 8, core: 2. Of those that a mesh axis runs over, the one named last changes fastest.
Arguments:
- aux_factors: bfloat16 [32, 1024, 2048], P('occ', ('vb', 'va')), may hold values from -0.59765625 to 0.59765625
- occ_energy: float32 [32], replicated, may hold values from -2 to -0.5
- vir_energy: float32 [1024], replicated, may hold values from 0.5 to 3
- occ_index: int32 [32], replicated, may hold values from 0 to 31, each once
- vir_index: int32 [1024], replicated, may hold values from 0 to 1023, each once
Outputs:
- gamma_aux: float32 [32, 1024, 2048], P('occ', ('vb', 'va'))
The draws below stay inside these ranges and needn't reach their ends.
Inputs may be any that keep to these rules, and one draw needn't show every extreme that they name: `occ_index`: each occupied table row appears exactly once. `vir_index`: each virtual table row appears exactly once.
All inputs are finite; a program needn't handle non-finite values.
Results may differ from the reference program's by a relative error of at most 0.0017.
Values may be sent and summed in bfloat16 or wider, within the bound.
A program may use at most 64 MiB of HBM per device.

```python
import jax
import jax.numpy as jnp
from jax import lax

V = 1024
NAUX = 2048
O_DEV = 1
STEPS = 4
O = 32


def level_of(rng, dims, cuts, low, largest):
    level = 1.0
    for axis_at, parts in cuts:
        draws = jax.random.uniform(jax.random.fold_in(jax.random.fold_in(rng, 6), axis_at), (parts,), jnp.float32, low / len(cuts), largest / len(cuts))
        level = level * jnp.repeat(jnp.exp(draws), dims[axis_at] // parts).reshape((-1,) + (1,) * (len(dims) - 1 - axis_at))
    return level


def bell_draw(rng, dims, width, reach, pieces=(), kind=jnp.bfloat16):
    drawn = jax.random.normal(rng, dims, jnp.float32) * width
    if len(pieces) > 0:
        drawn = level_of(rng, dims, pieces, -0.22, 0.18) * drawn
    return jnp.clip(drawn, min=-reach, max=reach).astype(kind)


def setup_inputs(seed: int = 0) -> dict:
    streams_of = jax.random.split(jax.random.key(seed), 6)
    return {
        "aux_factors": bell_draw(streams_of[0], (O, V, NAUX), 0.1, 0.59765625, ((0, 32), (1, 8))),
        "occ_energy": jnp.clip(jax.random.uniform(streams_of[1], (O,), jnp.float32, -2.0, -0.5), -2.0, -0.5),
        "vir_energy": jnp.clip(jax.random.uniform(streams_of[2], (V,), jnp.float32, 0.5, 3.0), 0.5, 3.0),
        "occ_index": jax.random.permutation(streams_of[3], O).astype(jnp.int32),
        "vir_index": jax.random.permutation(streams_of[4], V).astype(jnp.int32),
    }


def pair_term(resident, partner, eps_left, eps_right, eps_vir):
    kernel = jnp.einsum("iap,jbp->iajb", resident.astype(jnp.float32), partner.astype(jnp.float32))
    swapped = jnp.transpose(kernel, (0, 3, 2, 1))
    energy_gap = (eps_left[:, None, None, None] + eps_right[None, None, :, None]
                  - eps_vir[None, :, None, None] - eps_vir[None, None, None, :])
    weights = ((2.0 * kernel - swapped) / energy_gap).astype(jnp.bfloat16)
    return jnp.einsum("iajb,jbp->iap", weights.astype(jnp.float32), partner.astype(jnp.float32))


def reference(aux_factors, occ_energy, vir_energy, occ_index, vir_index):
    blocks_count = O // O_DEV
    eps_occ = occ_energy[occ_index].reshape(blocks_count, O_DEV)
    eps_vir = vir_energy[vir_index]
    blocks = aux_factors.reshape(blocks_count, O_DEV, V, NAUX)

    def one_block(home_block):
        resident = lax.dynamic_index_in_dim(blocks, home_block, 0, False)
        eps_left = lax.dynamic_index_in_dim(eps_occ, home_block, 0, False)
        accumulated = jnp.zeros((O_DEV, V, NAUX), jnp.float32)
        for distance in range(STEPS):
            other_block = (home_block - distance + blocks_count) % blocks_count
            partner = lax.dynamic_index_in_dim(blocks, other_block, 0, False)
            eps_right = lax.dynamic_index_in_dim(eps_occ, other_block, 0, False)
            accumulated = accumulated + pair_term(resident, partner, eps_left, eps_right, eps_vir)
        return accumulated

    result = lax.map(one_block, jnp.arange(blocks_count, dtype=jnp.int32))
    return result.reshape(O, V, NAUX)
```

```python
import functools

import jax
import jax.numpy as jnp
from jax import lax
from jax.experimental import pallas as pl
from jax.experimental.pallas import tpu as pltpu
from jax.sharding import PartitionSpec as P

MESH = pl.DeviceIdType.MESH
STEPS = 4
RING = 4
HALF = 64
QUARTER = 32
BLOCK = 128
NT = (((1,), (1,)), ((), ()))

ORDER = (
    (0, 0), (0, 3), (0, 1), (3, 0), (1, 0), (0, 2), (2, 0), (1, 3),
    (3, 3), (3, 1), (1, 1), (1, 2), (2, 3), (3, 2), (2, 1), (2, 2),
)
RELAYED = ((0, 1), (0, 0), (3, 0), (1, 0), (2, 0))


def pick(step, values):
    out = jnp.int32(values[0])
    for k, value in enumerate(values):
        if k and value != values[0]:
            out = jnp.where(step == k, jnp.int32(value), out)
    return out


def kernel(occ_count, aux, vir_e, vir_i, occ_e, occ_i, out, held, relay, acc, ev_row, ev_col,
           eo, send, recv, relay_send, relay_recv, pair_send, pair_recv, own_sem):
    occ = lax.axis_index("occ")
    va = lax.axis_index("va")
    vb = lax.axis_index("vb")
    x = va * 2 + vb // 2
    core = vb % 2
    y = occ % RING

    def at(occ_shift, x_shift=0, other_core=False):
        xs = (x + x_shift + RING) % RING
        cs = 1 - core if other_core else core
        return ((occ + occ_shift + occ_count) % occ_count, xs // 2, (xs % 2) * 2 + cs)

    peers = [at(0, 1), at(0, -1), at(1), at(-1), at(3), at(-3), at(4), at(-4), at(0, 0, True)]
    barrier = pltpu.get_barrier_semaphore()
    for peer in peers:
        pl.semaphore_signal(barrier, inc=1, device_id=peer, device_id_type=MESH)
    pl.semaphore_wait(barrier, len(peers))

    def rows(d, xr, h, q=None):
        start = h * HALF + (0 if q is None else q * QUARTER)
        return held.at[d, xr, pl.ds(start, HALF if q is None else QUARTER)]

    def own_rows(h):
        return aux.at[pl.ds(h * HALF, HALF)]

    def link(src, d, xr, h, q, whole, peer):
        return pltpu.make_async_remote_copy(
            src_ref=src, dst_ref=rows(d, xr, h, None if whole else q),
            send_sem=send.at[d, xr, h, q], recv_sem=recv.at[d, xr, h, q],
            device_id=peer, device_id_type=MESH)

    def arrived(d, xr, h):
        if d == 2 and (h == 0 or xr == 0) or xr == 2 and (h == 1 or d == 0):
            for q in range(2):
                link(rows(d, xr, h, q), d, xr, h, q, False, at(1)).wait_recv()
        else:
            link(rows(d, xr, h), d, xr, h, 0, True, at(1)).wait_recv()

    def source(d, xr, h):
        return own_rows(h) if d == 0 and xr == 0 else rows(d, xr, h)

    started = []

    def start(copy):
        copy.start()

    def send_x(d, xr, h):
        start(link(source(d, xr, h), d, 3, h, 0, True, at(0, 1)))
        start(link(source(d, xr, h), d, 1, h, 0, True, at(0, -1)))

    def relay_copy(k, src):
        return pltpu.make_async_remote_copy(
            src_ref=src, dst_ref=relay.at[k],
            send_sem=send.at[1, RELAYED[k][0], RELAYED[k][1], 0], recv_sem=relay_recv.at[k],
            device_id=at(-3), device_id_type=MESH)

    def send_y(xr, h):
        src = source(0, xr, h)
        k = RELAYED.index((xr, h))

        @pl.when(y == RING - 1)
        def _():
            relay_copy(k, src).start()

        @pl.when(y != RING - 1)
        def _():
            link(src, 1, xr, h, 0, True, at(1)).start()

        start(link(src, 3, xr, h, 0, True, at(3)))

    def relayed(k):
        xr, h = RELAYED[k]
        return pltpu.make_async_remote_copy(
            src_ref=relay.at[k], dst_ref=rows(1, xr, h),
            send_sem=relay_send.at[k], recv_sem=recv.at[1, xr, h, 0],
            device_id=at(4), device_id_type=MESH)

    def pass_relay(k):
        @pl.when(y == 0)
        def _():
            relay_copy(k, relay.at[k]).wait_recv()
            relayed(k).start()

    def x_far(d, xr, h):
        if xr == 3:
            start(link(rows(d, 3, h, 0), d, 2, h, 0, False, at(0, 1)))
        else:
            start(link(rows(d, 1, h, 1), d, 2, h, 1, False, at(0, -1)))

    def y_far(d, xr, h):
        if d == 1:
            start(link(rows(1, xr, h, 0), 2, xr, h, 0, False, at(1)))
        else:
            start(link(rows(3, xr, h, 1), 2, xr, h, 1, False, at(-1)))

    def pair(src, d, xr, h):
        return pltpu.make_async_remote_copy(
            src_ref=src, dst_ref=held.at[d, xr, pl.ds(BLOCK + h * HALF, HALF)],
            send_sem=pair_send.at[d, xr, h], recv_sem=pair_recv.at[d, xr, h],
            device_id=at(0, 0, True), device_id_type=MESH)

    def pair_start(d, xr, h):
        pair(source(d, xr, h), d, xr, h).start()

    def take(d, xr, h):
        arrived(d, xr, h)
        if h == 0:
            if d == 0:
                if xr != 2:
                    x_far(d, xr, h)
                send_y(xr, h)
            elif d != 2:
                y_far(d, xr, h)
        else:
            if xr == 0:
                if d != 2:
                    y_far(d, xr, h)
                send_x(d, xr, h)
            elif xr != 2:
                x_far(d, xr, h)
        pair_start(d, xr, h)

    def pair_ready(d, xr):
        for h in range(2):
            pair(source(d, xr, h), d, xr, h).wait_recv()

    own_copy = pltpu.make_async_copy(aux, held.at[0, 0, pl.ds(0, BLOCK)], own_sem)

    def ev_start():
        send_x(0, 0, 0)
        send_y(0, 1)
        own_copy.start()
        pair_start(0, 0, 0)
        pair_start(0, 0, 1)
        send_x(0, 0, 1)
        send_y(0, 0)

    def ev0():
        own_copy.wait()

    def ev1():
        take(0, 3, 0)
        take(0, 1, 0)
        take(3, 0, 1)
        pass_relay(0)
        take(1, 0, 1)
        take(0, 3, 1)

    def ev2():
        take(0, 1, 1)
        take(3, 0, 0)
        pass_relay(1)

    def ev3():
        take(2, 0, 1)
        take(0, 2, 0)
        take(1, 0, 0)

    def ev5():
        take(0, 2, 1)
        take(2, 0, 0)

    def ev7():
        pass_relay(2)
        take(1, 3, 1)
        take(1, 1, 1)
        take(3, 3, 0)
        take(1, 3, 0)

    def ev8():
        pass_relay(3)
        take(3, 3, 1)

    def ev9():
        take(3, 1, 1)
        take(3, 1, 0)

    def ev10():
        take(1, 1, 0)

    def ev11():
        pass_relay(4)
        take(2, 3, 1)
        take(2, 1, 1)
        take(3, 2, 0)
        take(1, 2, 0)
        take(1, 2, 1)

    def ev12():
        take(2, 3, 0)

    def ev13():
        take(3, 2, 1)

    def ev14():
        take(2, 1, 0)

    def ev15():
        take(2, 2, 0)
        take(2, 2, 1)

    events = {0: ev0, 1: ev1, 2: ev2, 3: ev3, 5: ev5, 7: ev7, 8: ev8, 9: ev9, 10: ev10, 11: ev11,
              12: ev12, 13: ev13, 14: ev14, 15: ev15}

    ev_start()

    acc[...] = jnp.zeros_like(acc)
    lookup_energies(occ, occ_count, x, core, vir_e, vir_i, occ_e, occ_i, ev_row, ev_col, eo)

    def tile(step, carry):
        for k, event in events.items():
            pl.when(step == k)(event)
        for k, (d, xr) in enumerate(ORDER):
            pl.when(step == k)(functools.partial(pair_ready, d, xr))
        d = pick(step, [o[0] for o in ORDER])
        xr = pick(step, [o[1] for o in ORDER])
        coul = lax.dot_general(held[0, 0, 0:BLOCK], held[d, xr], NT, preferred_element_type=jnp.float32)
        swap = lax.dot_general(held[d, 0, 0:BLOCK], held[0, xr], NT, preferred_element_type=jnp.float32)
        xs = (x + xr) % RING
        near = ev_row[pl.ds((xs % 2) * 4 + core * 2 + xs // 2, 1), :]
        far = ev_row[pl.ds((xs % 2) * 4 + (1 - core) * 2 + xs // 2, 1), :]
        base = eo[pl.ds(0, 1), :] + eo[pl.ds(d, 1), :]
        left = jnp.broadcast_to(base, (BLOCK, BLOCK)) - ev_col[...]
        gap = jnp.concatenate([left - near, left - far], axis=1)
        weights = ((2.0 * coul - swap) / gap).astype(jnp.bfloat16)
        for c in range(4):
            cols = pl.ds(c * 512, 512)
            acc[:, cols] += jnp.dot(weights, held[d, xr, :, cols], preferred_element_type=jnp.float32)
        return carry

    lax.fori_loop(0, len(ORDER), tile, 0)
    out[...] = acc[...]

    for d in range(STEPS):
        for xr in range(RING):
            for h in range(2):
                pair(source(d, xr, h), d, xr, h).wait_send()
                if d == 0 and xr == 0:
                    continue
                if d == 2 and (h == 0 or xr == 0) or xr == 2 and (h == 1 or d == 0):
                    for q in range(2):
                        link(rows(d, xr, h, q), d, xr, h, q, False, at(1)).wait_send()
                else:
                    link(rows(d, xr, h), d, xr, h, 0, True, at(1)).wait_send()

    @pl.when(y == 0)
    def _():
        for k in range(len(RELAYED)):
            relayed(k).wait_send()


def lookup_energies(occ, occ_count, x, core, vir_e, vir_i, occ_e, occ_i, ev_row, ev_col, eo):
    groups = vir_e.shape[0]
    lanes = lax.broadcasted_iota(jnp.int32, occ_e.shape, 1)
    for d in range(STEPS):
        mine = lanes == (occ - d + occ_count) % occ_count
        index = jnp.sum(jnp.where(mine, occ_i[...], 0), axis=1, keepdims=True)
        value = jnp.sum(jnp.where(lanes == index, occ_e[...], 0.0), axis=1, keepdims=True)
        eo[pl.ds(d, 1), :] = jnp.broadcast_to(value, (1, BLOCK))
    ev_row[...] = jnp.zeros_like(ev_row)
    place = lax.broadcasted_iota(jnp.int32, (BLOCK, BLOCK), 0)

    def group(g, carry):
        table = jnp.transpose(jnp.broadcast_to(vir_e[pl.ds(g, 1), :], (BLOCK, BLOCK)))
        for r in range(groups):
            hit = place + g * BLOCK == jnp.broadcast_to(vir_i[pl.ds(r, 1), :], (BLOCK, BLOCK))
            ev_row[pl.ds(r, 1), :] += jnp.sum(jnp.where(hit, table, 0.0), axis=0, keepdims=True)
        return carry

    lax.fori_loop(0, groups, group, 0)
    mine = ev_row[pl.ds((x % 2) * 4 + core * 2 + x // 2, 1), :]
    ev_col[...] = jnp.transpose(jnp.broadcast_to(mine, (BLOCK, BLOCK)))


def per_device(aux_factors, occ_energy, vir_energy, occ_index, vir_index):
    occ_count = lax.axis_size("occ")
    _, width, aux_width = aux_factors.shape
    groups = vir_energy.shape[0] // BLOCK
    vmem = pl.BlockSpec(memory_space=pltpu.VMEM)
    dma = pltpu.SemaphoreType.DMA
    result = pl.pallas_call(
        functools.partial(kernel, occ_count),
        out_shape=jax.ShapeDtypeStruct((width, aux_width), jnp.float32),
        in_specs=[pl.BlockSpec(memory_space=pl.ANY)] + [vmem] * 4,
        out_specs=vmem,
        scratch_shapes=[
            pltpu.VMEM((STEPS, RING, 2 * BLOCK, aux_width), jnp.bfloat16),
            pltpu.VMEM((len(RELAYED), HALF, aux_width), jnp.bfloat16),
            pltpu.VMEM((width, aux_width), jnp.float32),
            pltpu.VMEM((groups, BLOCK), jnp.float32),
            pltpu.VMEM((BLOCK, BLOCK), jnp.float32),
            pltpu.VMEM((8, BLOCK), jnp.float32),
            dma((STEPS, RING, 2, 2)),
            dma((STEPS, RING, 2, 2)),
            dma((len(RELAYED),)),
            dma((len(RELAYED),)),
            dma((STEPS, RING, 2)),
            dma((STEPS, RING, 2)),
            dma,
        ],
        compiler_params=pltpu.CompilerParams(
            collective_id=0, has_side_effects=True, vmem_limit_bytes=40 << 20),
        cost_estimate=pl.CostEstimate(
            flops=6 * STEPS * width * 8 * BLOCK * aux_width, bytes_accessed=2 << 20, transcendentals=0),
    )(
        aux_factors.reshape(width, aux_width),
        vir_energy.reshape(groups, BLOCK),
        vir_index.reshape(groups, BLOCK),
        occ_energy.reshape(1, -1),
        occ_index.reshape(1, -1),
    )
    return result.reshape(1, width, aux_width)


def solution(mesh):
    return jax.shard_map(
        per_device,
        mesh=mesh,
        in_specs=(P("occ", ("vb", "va"), None), P(), P(), P(), P()),
        out_specs=P("occ", ("vb", "va"), None),
        check_vma=False,
    )
```

```python
import functools

import jax
import jax.numpy as jnp
from jax import lax
from jax.experimental import pallas as pl
from jax.experimental.pallas import tpu as pltpu
from jax.sharding import PartitionSpec as P

LOGICAL = pl.DeviceIdType.LOGICAL
STEPS = 4
RING = 4
BLOCK = 128
PIECES = 4
FIRST = PIECES // 2
PIECE = BLOCK // PIECES
NT = (((1,), (1,)), ((), ()))

ORDER = (
    (0, 0),
    (0, 1),
    (3, 0),
    (0, 3),
    (1, 0),
    (0, 2),
    (3, 1),
    (1, 1),
    (3, 3),
    (2, 0),
    (1, 3),
    (2, 1),
    (3, 2),
    (1, 2),
    (2, 3),
    (2, 2),
)
PLAN = (
    (),
    ((0,), (0, 1, 0), (3, 0, 2), (1,), (0, 1, 1), (0, 3, 1), (0, 1, 2), (0, 3, 2), (0, 3, 3), (3,), (0, 1, 3), (2,), (3, 0, 0), (3, 0, 3), (0, 3, 0), (1, 0, 3), (3, 0, 1), (1, 0, 2), (6,), (3, 3, 2), (3, 1, 2), (3, 1, 0), (0, 2, 2), (7,), (0, 2, 1), (1, 0, 1), (1, 0, 0)),
    ((4,), (3, 3, 3), (0, 2, 3)),
    ((3, 1, 3), (5,), (0, 2, 0), (1, 1, 0), (2, 0, 3), (9,), (1, 1, 1), (3, 1, 1)),
    ((1, 3, 3),),
    ((1, 3, 0), (2, 0, 2), (1, 1, 3), (1, 3, 2), (1, 1, 2), (2, 0, 1), (8,), (3, 3, 1)),
    ((3, 3, 0),),
    ((1, 3, 1), (3, 2, 3), (3, 2, 1), (3, 2, 2), (2, 1, 3), (2, 0, 0)),
    (),
    ((1, 2, 0), (2, 1, 2), (2, 3, 2), (2, 1, 0), (2, 1, 1), (2, 3, 3)),
    ((1, 2, 1), (3, 2, 0), (1, 2, 3), (1, 2, 2)),
    ((2, 3, 1), (2, 2, 3), (2, 3, 0)),
    ((2, 2, 1), (2, 2, 2), (2, 2, 0)),
    (),
    (),
    (),
)
RELAYED = (
    tuple((0, q) for q in range(FIRST, PIECES))
    + tuple((0, q) for q in range(FIRST))
    + tuple((xr, q) for xr in (3, 1, 2) for q in range(FIRST))
)


def pick(step, values):
    out = jnp.int32(values[0])
    for k, value in enumerate(values):
        if k and value != values[0]:
            out = jnp.where(step == k, jnp.int32(value), out)
    return out


def kernel(occ_count, aux, vir_e_in, vir_i_in, occ_e_in, occ_i_in, out, held, relay, vir_e, vir_i, occ_e, occ_i,
           ev_row, ev_col, eo, weights, send, recv, relay_send, relay_recv, pair_send, pair_recv, own_sem):
    occ = lax.axis_index("occ")
    va = lax.axis_index("va")
    vb = lax.axis_index("vb")
    x = va * 2 + vb // 2
    core = vb % 2
    y = occ % RING

    va_count = lax.axis_size("va")
    vb_count = lax.axis_size("vb")

    def device(occ_shift, x_shift=0, other_core=False):
        xs = (x + x_shift + RING) % RING
        cs = 1 - core if other_core else core
        far = (occ + occ_shift + occ_count) % occ_count
        return (far * va_count + xs // 2) * vb_count + (xs % 2) * 2 + cs

    right, left_side = device(0, 1), device(0, -1)
    ahead = {k: device(k) for k in (1, -1, 3, -3, 4, -4)}
    partner = device(0, 0, True)
    first_row = y == 0
    last_row = y == RING - 1

    tables = [
        pltpu.make_async_copy(src, dst, own_sem.at[1 + k])
        for k, (src, dst) in enumerate(((vir_e_in, vir_e), (vir_i_in, vir_i), (occ_e_in, occ_e), (occ_i_in, occ_i)))
    ]
    own_copy = pltpu.make_async_copy(aux, held.at[0, 0, pl.ds(0, BLOCK)], own_sem.at[0])
    peers = [right, left_side, *ahead.values(), partner]
    barrier = pltpu.get_barrier_semaphore()
    for peer in peers:
        pl.semaphore_signal(barrier, inc=1, device_id=peer, device_id_type=LOGICAL)
    own_copy.start()
    for table in tables:
        table.start()
    pl.semaphore_wait(barrier, len(peers))

    def rows(d, xr, q):
        return held.at[d, xr, pl.ds(q * PIECE, PIECE)]

    def source(d, xr, q):
        return aux.at[pl.ds(q * PIECE, PIECE)] if d == 0 and xr == 0 else rows(d, xr, q)

    def link(src, d, xr, q, peer):
        return pltpu.make_async_remote_copy(
            src_ref=src, dst_ref=rows(d, xr, q), send_sem=send.at[d, xr, q], recv_sem=recv.at[d, xr, q],
            device_id=peer, device_id_type=LOGICAL)

    def relay_in(k, src):
        xr, q = RELAYED[k]
        return pltpu.make_async_remote_copy(
            src_ref=src, dst_ref=relay.at[k], send_sem=send.at[1, xr, q], recv_sem=relay_recv.at[k],
            device_id=ahead[-3], device_id_type=LOGICAL)

    def relay_out(k):
        xr, q = RELAYED[k]
        return pltpu.make_async_remote_copy(
            src_ref=relay.at[k], dst_ref=rows(1, xr, q), send_sem=relay_send.at[k], recv_sem=recv.at[1, xr, q],
            device_id=ahead[4], device_id_type=LOGICAL)

    def send_x(d, q):
        link(source(d, 0, q), d, 3, q, right).start()
        link(source(d, 0, q), d, 1, q, left_side).start()

    def send_y(xr, q):
        src = source(0, xr, q)

        @pl.when(last_row)
        def _():
            relay_in(RELAYED.index((xr, q)), src).start()

        @pl.when(jnp.logical_not(last_row))
        def _():
            link(src, 1, xr, q, ahead[1]).start()

        link(src, 3, xr, q, ahead[3]).start()

    def pass_relay(k):
        @pl.when(first_row)
        def _():
            relay_in(k, relay.at[k]).wait_recv()
            relay_out(k).start()

    def x_far(d, xr, q):
        if xr == 3 and q % 2 == 0:
            link(rows(d, xr, q), d, 2, q, right).start()
        if xr == 1 and q % 2 == 1:
            link(rows(d, xr, q), d, 2, q, left_side).start()

    def y_far(d, xr, q):
        if d == 1 and q % 2 == 0:
            link(rows(d, xr, q), 2, xr, q, ahead[1]).start()
        if d == 3 and q % 2 == 1:
            link(rows(d, xr, q), 2, xr, q, ahead[-1]).start()

    def pair(d, xr, h):
        span = pl.ds(h * FIRST * PIECE, FIRST * PIECE)
        src = aux.at[span] if d == 0 and xr == 0 else held.at[d, xr, span]
        return pltpu.make_async_remote_copy(
            src_ref=src, dst_ref=held.at[d, xr, pl.ds(BLOCK + h * FIRST * PIECE, FIRST * PIECE)],
            send_sem=pair_send.at[d, xr, h], recv_sem=pair_recv.at[d, xr, h],
            device_id=partner, device_id_type=LOGICAL)

    missing = {(d, xr, h): FIRST for d in range(STEPS) for xr in range(RING) for h in range(2)}

    def take(d, xr, q):
        link(rows(d, xr, q), d, xr, q, ahead[1]).wait_recv()
        if q < FIRST:
            if d == 0:
                x_far(d, xr, q)
                send_y(xr, q)
            else:
                y_far(d, xr, q)
        elif xr == 0:
            y_far(d, xr, q)
            send_x(d, q)
        else:
            x_far(d, xr, q)
        h = q // FIRST
        missing[d, xr, h] -= 1
        if missing[d, xr, h] == 0:
            pair(d, xr, h).start()

    def pair_ready(d, xr):
        for h in range(2):
            pair(d, xr, h).wait_recv()

    def events(k):
        for item in PLAN[k]:
            if len(item) == 1:
                pass_relay(*item)
            else:
                take(*item)
        pair_ready(*ORDER[k])

    for q in range(FIRST):
        send_x(0, q)
        send_y(0, FIRST + q)
    for q in range(FIRST):
        send_x(0, FIRST + q)
        send_y(0, q)
    pair(0, 0, 0).start()
    pair(0, 0, 1).start()

    out[...] = jnp.zeros_like(out)
    for table in tables:
        table.wait()
    lookup_energies(occ, occ_count, x, core, vir_e, vir_i, occ_e, occ_i, ev_row, ev_col, eo)
    own_copy.wait()

    def tile_of(step):
        if isinstance(step, int):
            return ORDER[step]
        return pick(step, [o[0] for o in ORDER]), pick(step, [o[1] for o in ORDER])

    def add_gradient(step):
        d, xr = tile_of(step)
        held_weights = weights[...]
        for c in range(4):
            cols = pl.ds(c * 512, 512)
            out[:, cols] += jnp.dot(held_weights, held[d, xr, :, cols], preferred_element_type=jnp.float32)

    def tile(step, carry):
        for k in range(len(ORDER)):
            pl.when(step == k)(functools.partial(events, k))
        add_gradient(step - jnp.minimum(step, 1))
        d, xr = tile_of(step)
        coul = lax.dot_general(held[0, 0, 0:BLOCK], held[d, xr], NT, preferred_element_type=jnp.float32)
        swap = lax.dot_general(held[d, 0, 0:BLOCK], held[0, xr], NT, preferred_element_type=jnp.float32)
        xs = (x + xr) % RING
        near = ev_row[pl.ds((xs % 2) * 4 + core * 2 + xs // 2, 1), :]
        far = ev_row[pl.ds((xs % 2) * 4 + (1 - core) * 2 + xs // 2, 1), :]
        base = eo[pl.ds(0, 1), :] + eo[pl.ds(d, 1), :]
        left = jnp.broadcast_to(base, (BLOCK, BLOCK)) - ev_col[...]
        gap = jnp.concatenate([left - near, left - far], axis=1)
        weights[...] = ((2.0 * coul - swap) / gap).astype(jnp.bfloat16)
        return carry

    weights[...] = jnp.zeros_like(weights)
    lax.fori_loop(0, len(ORDER), tile, 0)
    add_gradient(len(ORDER) - 1)

    for d in range(STEPS):
        for xr in range(RING):
            for h in range(2):
                pair(d, xr, h).wait_send()
            if d or xr:
                for q in range(PIECES):
                    link(rows(d, xr, q), d, xr, q, ahead[1]).wait_send()

    @pl.when(first_row)
    def _():
        for k in range(len(RELAYED)):
            relay_out(k).wait_send()


def lookup_energies(occ, occ_count, x, core, vir_e, vir_i, occ_e, occ_i, ev_row, ev_col, eo):
    groups = vir_e.shape[0]
    lanes = lax.broadcasted_iota(jnp.int32, occ_e.shape, 1)
    for d in range(STEPS):
        mine = lanes == (occ - d + occ_count) % occ_count
        index = jnp.sum(jnp.where(mine, occ_i[...], 0), axis=1, keepdims=True)
        value = jnp.sum(jnp.where(lanes == index, occ_e[...], 0.0), axis=1, keepdims=True)
        eo[pl.ds(d, 1), :] = jnp.broadcast_to(value, (1, BLOCK))
    ev_row[...] = jnp.zeros_like(ev_row)
    place = lax.broadcasted_iota(jnp.int32, (BLOCK, BLOCK), 0)

    def group(g, carry):
        table = jnp.transpose(jnp.broadcast_to(vir_e[pl.ds(g, 1), :], (BLOCK, BLOCK)))
        for r in range(groups):
            hit = place + g * BLOCK == jnp.broadcast_to(vir_i[pl.ds(r, 1), :], (BLOCK, BLOCK))
            ev_row[pl.ds(r, 1), :] += jnp.sum(jnp.where(hit, table, 0.0), axis=0, keepdims=True)
        return carry

    lax.fori_loop(0, groups, group, 0)
    mine = ev_row[pl.ds((x % 2) * 4 + core * 2 + x // 2, 1), :]
    ev_col[...] = jnp.transpose(jnp.broadcast_to(mine, (BLOCK, BLOCK)))


def per_device(aux_factors, occ_energy, vir_energy, occ_index, vir_index):
    occ_count = lax.axis_size("occ")
    _, width, aux_width = aux_factors.shape
    groups = vir_energy.shape[0] // BLOCK
    dma = pltpu.SemaphoreType.DMA
    in_hbm = functools.partial(pltpu.with_memory_space_constraint, memory_space=pltpu.HBM)
    result = pl.pallas_call(
        functools.partial(kernel, occ_count),
        out_shape=jax.ShapeDtypeStruct((width, aux_width), jnp.float32),
        in_specs=[pl.BlockSpec(memory_space=pltpu.HBM)] * 5,
        out_specs=pl.BlockSpec(memory_space=pltpu.VMEM),
        scratch_shapes=[
            pltpu.VMEM((STEPS, RING, 2 * BLOCK, aux_width), jnp.bfloat16),
            pltpu.VMEM((len(RELAYED), PIECE, aux_width), jnp.bfloat16),
            pltpu.VMEM((groups, BLOCK), jnp.float32),
            pltpu.VMEM((groups, BLOCK), jnp.int32),
            pltpu.VMEM((1, occ_count), jnp.float32),
            pltpu.VMEM((1, occ_count), jnp.int32),
            pltpu.VMEM((groups, BLOCK), jnp.float32),
            pltpu.VMEM((BLOCK, BLOCK), jnp.float32),
            pltpu.VMEM((8, BLOCK), jnp.float32),
            pltpu.VMEM((BLOCK, 2 * BLOCK), jnp.bfloat16),
            dma((STEPS, RING, PIECES)),
            dma((STEPS, RING, PIECES)),
            dma((len(RELAYED),)),
            dma((len(RELAYED),)),
            dma((STEPS, RING, 2)),
            dma((STEPS, RING, 2)),
            dma((5,)),
        ],
        compiler_params=pltpu.CompilerParams(
            collective_id=0, has_side_effects=True, vmem_limit_bytes=40 << 20),
        cost_estimate=pl.CostEstimate(
            flops=6 * STEPS * width * 8 * BLOCK * aux_width, bytes_accessed=2 << 20, transcendentals=0),
    )(
        in_hbm(aux_factors.reshape(width, aux_width)),
        in_hbm(vir_energy.reshape(groups, BLOCK)),
        in_hbm(vir_index.reshape(groups, BLOCK)),
        in_hbm(occ_energy.reshape(1, occ_count)),
        in_hbm(occ_index.reshape(1, occ_count)),
    )
    return result.reshape(1, width, aux_width)


def solution(mesh):
    return jax.shard_map(
        per_device,
        mesh=mesh,
        in_specs=(P("occ", ("vb", "va"), None), P(), P(), P(), P()),
        out_specs=P("occ", ("vb", "va"), None),
        check_vma=False,
    )
```

```python
import functools

import jax
import jax.numpy as jnp
from jax import lax
from jax.experimental import pallas as pl
from jax.experimental.pallas import tpu as pltpu
from jax.sharding import PartitionSpec as P

LOGICAL = pl.DeviceIdType.LOGICAL
STEPS = 4
RING = 4
BLOCK = 128
PIECES = 4
FIRST = PIECES // 2
PIECE = BLOCK // PIECES
NT = (((1,), (1,)), ((), ()))

ORDER = (
    (0, 1),
    (0, 0),
    (3, 0),
    (1, 0),
    (3, 1),
    (0, 3),
    (3, 3),
    (1, 3),
    (1, 1),
    (0, 2),
    (2, 0),
    (3, 2),
    (1, 2),
    (2, 1),
    (2, 3),
    (2, 2),
)
PLAN = (
    (("T", 0, 3, 0), ("T", 0, 1, 0), ("R", 0), ("T", 3, 0, 2), ("XF", 0, 3, 0), ("T", 0, 1, 1), ("Y", 3, 0), ("R", 1), ("R", 2), ("Y", 1, 1), ("T", 3, 0, 3), ("XF", 0, 1, 1), ("T", 1, 0, 2), ("R", 3), ("YF", 1, 0, 2), ("T", 0, 3, 1), ("Y", 3, 1), ("T", 3, 0, 0), ("T", 0, 1, 2), ("T", 0, 1, 3), ("X", 3, 2), ("T", 0, 3, 3), ("T", 0, 3, 2), ("XF", 0, 3, 2), ("T", 1, 0, 3), ("X", 3, 3), ("R", 4), ("YF", 3, 0, 3), ("T", 3, 0, 1), ("T", 0, 2, 0), ("X", 1, 3), ("T", 3, 3, 0), ("T", 1, 0, 0), ("R", 7), ("Y", 1, 0), ("T", 3, 3, 2), ("X", 1, 2), ("Y", 2, 0), ("T", 3, 1, 2), ("T", 1, 3, 0), ("T", 1, 0, 1), ("R", 5), ("T", 3, 1, 1), ("XF", 0, 1, 3), ("R", 6), ("XF", 3, 3, 2), ("T", 0, 2, 1), ("T", 0, 2, 2), ("Y", 2, 1), ("T", 3, 1, 3), ("T", 1, 1, 1), ("T", 3, 3, 3), ("T", 1, 1, 3), ("T", 3, 3, 1)),
    (("XF", 3, 1, 3), ("T", 1, 1, 2), ("YF", 1, 0, 0), ("T", 2, 0, 3), ("T", 2, 0, 2)),
    (("X", 2, 2), ("T", 3, 1, 0), ("YF", 3, 0, 1), ("R", 8)),
    (("T", 1, 3, 2), ("X", 2, 3), ("T", 0, 2, 3)),
    (("YF", 3, 1, 1), ("T", 1, 3, 1), ("R", 9), ("XF", 1, 1, 3), ("T", 1, 1, 0), ("T", 3, 2, 0), ("YF", 1, 1, 0), ("YF", 1, 3, 0), ("T", 3, 2, 3), ("T", 1, 3, 3), ("YF", 3, 3, 1), ("XF", 1, 3, 2)),
    (("T", 3, 2, 1), ("T", 3, 2, 2)),
    (("T", 1, 2, 0), ("T", 2, 1, 2), ("YF", 1, 2, 0), ("T", 2, 3, 2), ("XF", 2, 3, 2), ("YF", 3, 2, 1), ("T", 2, 0, 0), ("T", 2, 0, 1)),
    (),
    (("T", 2, 1, 3), ("T", 1, 2, 1), ("XF", 2, 1, 3), ("T", 2, 1, 0)),
    (),
    (("T", 2, 1, 1), ("T", 1, 2, 3), ("T", 1, 2, 2), ("T", 2, 3, 3)),
    (("T", 2, 3, 0), ("T", 2, 3, 1)),
    (("T", 2, 2, 1), ("T", 2, 2, 2), ("T", 2, 2, 3), ("T", 2, 2, 0)),
    (),
    (),
    (),
)
RELAYED = (
    tuple((0, q) for q in range(FIRST, PIECES))
    + tuple((0, q) for q in range(FIRST))
    + tuple((xr, q) for xr in (3, 1, 2) for q in range(FIRST))
)


def pick(step, values):
    out = jnp.int32(values[0])
    for k, value in enumerate(values):
        if k and value != values[0]:
            out = jnp.where(step == k, jnp.int32(value), out)
    return out


def kernel(occ_count, aux, vir_e_in, vir_i_in, occ_e_in, occ_i_in, out, held, relay, vir_e, vir_i, occ_e, occ_i,
           ev_row, ev_col, eo, weights, mine, swaps, send, recv, relay_send, relay_recv, pair_send, pair_recv, own_sem, mine_sem):
    occ = lax.axis_index("occ")
    va = lax.axis_index("va")
    vb = lax.axis_index("vb")
    x = va * 2 + vb // 2
    core = vb % 2
    y = occ % RING

    va_count = lax.axis_size("va")
    vb_count = lax.axis_size("vb")

    def device(occ_shift, x_shift=0, other_core=False):
        xs = (x + x_shift + RING) % RING
        cs = 1 - core if other_core else core
        far = (occ + occ_shift + occ_count) % occ_count
        return (far * va_count + xs // 2) * vb_count + (xs % 2) * 2 + cs

    right, left_side = device(0, 1), device(0, -1)
    ahead = {k: device(k) for k in (1, -1, 3, -3, 4, -4)}
    partner = device(0, 0, True)
    first_row = y == 0
    last_row = y == RING - 1

    tables = [
        pltpu.make_async_copy(src, dst, own_sem.at[1 + k])
        for k, (src, dst) in enumerate(((vir_e_in, vir_e), (vir_i_in, vir_i), (occ_e_in, occ_e), (occ_i_in, occ_i)))
    ]
    own_copy = pltpu.make_async_copy(aux, held.at[0, 0, pl.ds(0, BLOCK)], own_sem.at[0])
    first_mine = pltpu.make_async_copy(aux, mine.at[pl.ds(0, BLOCK)], own_sem.at[5])
    peers = [right, left_side, *ahead.values(), partner]
    barrier = pltpu.get_barrier_semaphore()
    for peer in peers:
        pl.semaphore_signal(barrier, inc=1, device_id=peer, device_id_type=LOGICAL)
    own_copy.start()
    first_mine.start()
    for table in tables:
        table.start()
    pl.semaphore_wait(barrier, len(peers))

    def rows(d, xr, q):
        return held.at[d, xr, pl.ds(q * PIECE, PIECE)]

    def source(d, xr, q):
        return aux.at[pl.ds(q * PIECE, PIECE)] if d == 0 and xr == 0 else rows(d, xr, q)

    def link(src, d, xr, q, peer):
        return pltpu.make_async_remote_copy(
            src_ref=src, dst_ref=rows(d, xr, q), send_sem=send.at[d, xr, q], recv_sem=recv.at[d, xr, q],
            device_id=peer, device_id_type=LOGICAL)

    def relay_in(k, src):
        xr, q = RELAYED[k]
        return pltpu.make_async_remote_copy(
            src_ref=src, dst_ref=relay.at[k], send_sem=send.at[1, xr, q], recv_sem=relay_recv.at[k],
            device_id=ahead[-3], device_id_type=LOGICAL)

    def relay_out(k):
        xr, q = RELAYED[k]
        return pltpu.make_async_remote_copy(
            src_ref=relay.at[k], dst_ref=rows(1, xr, q), send_sem=relay_send.at[k], recv_sem=recv.at[1, xr, q],
            device_id=ahead[4], device_id_type=LOGICAL)

    def send_x(d, q):
        link(source(d, 0, q), d, 3, q, right).start()
        link(source(d, 0, q), d, 1, q, left_side).start()

    def send_y(xr, q):
        src = source(0, xr, q)

        @pl.when(last_row)
        def _():
            relay_in(RELAYED.index((xr, q)), src).start()

        @pl.when(jnp.logical_not(last_row))
        def _():
            link(src, 1, xr, q, ahead[1]).start()

        link(src, 3, xr, q, ahead[3]).start()

    def pass_relay(k):
        @pl.when(first_row)
        def _():
            relay_in(k, relay.at[k]).wait_recv()
            relay_out(k).start()

    def x_far(d, xr, q):
        if xr == 3 and q % 2 == 0:
            link(rows(d, xr, q), d, 2, q, right).start()
        if xr == 1 and q % 2 == 1:
            link(rows(d, xr, q), d, 2, q, left_side).start()

    def y_far(d, xr, q):
        if d == 1 and q % 2 == 0:
            link(rows(d, xr, q), 2, xr, q, ahead[1]).start()
        if d == 3 and q % 2 == 1:
            link(rows(d, xr, q), 2, xr, q, ahead[-1]).start()

    def pair(d, xr, h):
        span = pl.ds(h * FIRST * PIECE, FIRST * PIECE)
        src = aux.at[span] if d == 0 and xr == 0 else held.at[d, xr, span]
        return pltpu.make_async_remote_copy(
            src_ref=src, dst_ref=held.at[d, xr, pl.ds(BLOCK + h * FIRST * PIECE, FIRST * PIECE)],
            send_sem=pair_send.at[d, xr, h], recv_sem=pair_recv.at[d, xr, h],
            device_id=partner, device_id_type=LOGICAL)

    missing = {(d, xr, h): FIRST for d in range(STEPS) for xr in range(RING) for h in range(2)}

    def take(d, xr, q):
        link(rows(d, xr, q), d, xr, q, ahead[1]).wait_recv()
        h = q // FIRST
        missing[d, xr, h] -= 1
        if missing[d, xr, h] == 0:
            pair(d, xr, h).start()
            if d % 2 and xr == 0 and missing[d, 0, 1 - h] == 0:
                mine_copy(1 + d // 2).start()

    def mine_copy(k):
        return pltpu.make_async_copy(
            held.at[(0, 1, 3)[k], 0, pl.ds(0, BLOCK)], mine.at[pl.ds(k * BLOCK, BLOCK)], mine_sem.at[k])

    waited = []

    def pair_ready(d, xr):
        for h in range(2):
            pair(d, xr, h).wait_recv()
        if not waited:
            waited.append(True)
            mine_copy(1).wait()
            mine_copy(2).wait()

    actions = {"T": take, "R": pass_relay, "X": send_x, "Y": send_y, "XF": x_far, "YF": y_far}

    def events(k):
        for what, *item in PLAN[k]:
            actions[what](*item)
        pair_ready(*ORDER[k])

    for q in range(FIRST):
        send_x(0, q)
        send_y(0, FIRST + q)
    for q in range(FIRST):
        send_x(0, FIRST + q)
        send_y(0, q)
    pair(0, 0, 0).start()
    pair(0, 0, 1).start()

    out[...] = jnp.zeros_like(out)
    for table in tables:
        table.wait()
    lookup_energies(occ, occ_count, x, core, vir_e, vir_i, occ_e, occ_i, ev_row, ev_col, eo)
    own_copy.wait()
    first_mine.wait()

    def tile_of(step):
        if isinstance(step, int):
            return ORDER[step]
        return pick(step, [o[0] for o in ORDER]), pick(step, [o[1] for o in ORDER])

    def add_gradient(step):
        d, xr = tile_of(step)
        held_weights = weights[...]
        for c in range(4):
            cols = pl.ds(c * 512, 512)
            out[:, cols] += jnp.dot(held_weights, held[d, xr, :, cols], preferred_element_type=jnp.float32)

    def gap_of(d, xr):
        xs = (x + xr) % RING
        near = ev_row[pl.ds((xs % 2) * 4 + core * 2 + xs // 2, 1), :]
        far = ev_row[pl.ds((xs % 2) * 4 + (1 - core) * 2 + xs // 2, 1), :]
        base = eo[pl.ds(0, 1), :] + eo[pl.ds(d, 1), :]
        left = jnp.broadcast_to(base, (BLOCK, BLOCK)) - ev_col[...]
        return jnp.concatenate([left - near, left - far], axis=1)

    def product(left, d, xr):
        return lax.dot_general(left, held[d, xr], NT, preferred_element_type=jnp.float32)

    def tile(step, carry):
        for k in range(len(ORDER)):
            pl.when(step == k)(functools.partial(events, k))
        before = step - jnp.minimum(step, 1)
        d, xr = tile_of(step)

        @pl.when(d == 0)
        def _():
            add_gradient(before)
            coul = product(mine[...], 0, xr)
            swaps[0, xr] = coul[BLOCK:2 * BLOCK]
            swaps[1, xr] = coul[2 * BLOCK:]
            coul = coul[:BLOCK]
            weights[...] = ((2.0 * coul - coul) / gap_of(0, xr)).astype(jnp.bfloat16)

        @pl.when(d % 2 == 1)
        def _():
            add_gradient(before)
            coul = product(mine[0:BLOCK], d, xr)
            weights[...] = ((2.0 * coul - swaps[d // 2, xr]) / gap_of(d, xr)).astype(jnp.bfloat16)

        @pl.when(d == 2)
        def _():
            add_gradient(before)
            coul = product(mine[0:BLOCK], d, xr)
            swap = product(held[2, 0, 0:BLOCK], 0, xr)
            weights[...] = ((2.0 * coul - swap) / gap_of(d, xr)).astype(jnp.bfloat16)

        return carry

    weights[...] = jnp.zeros_like(weights)
    lax.fori_loop(0, len(ORDER), tile, 0)
    add_gradient(len(ORDER) - 1)

    for d in range(STEPS):
        for xr in range(RING):
            for h in range(2):
                pair(d, xr, h).wait_send()
            if d or xr:
                for q in range(PIECES):
                    link(rows(d, xr, q), d, xr, q, ahead[1]).wait_send()

    @pl.when(first_row)
    def _():
        for k in range(len(RELAYED)):
            relay_out(k).wait_send()


def lookup_energies(occ, occ_count, x, core, vir_e, vir_i, occ_e, occ_i, ev_row, ev_col, eo):
    groups = vir_e.shape[0]
    lanes = lax.broadcasted_iota(jnp.int32, occ_e.shape, 1)
    for d in range(STEPS):
        mine = lanes == (occ - d + occ_count) % occ_count
        index = jnp.sum(jnp.where(mine, occ_i[...], 0), axis=1, keepdims=True)
        value = jnp.sum(jnp.where(lanes == index, occ_e[...], 0.0), axis=1, keepdims=True)
        eo[pl.ds(d, 1), :] = jnp.broadcast_to(value, (1, BLOCK))
    ev_row[...] = jnp.zeros_like(ev_row)
    place = lax.broadcasted_iota(jnp.int32, (BLOCK, BLOCK), 0)

    def group(g, carry):
        table = jnp.transpose(jnp.broadcast_to(vir_e[pl.ds(g, 1), :], (BLOCK, BLOCK)))
        for r in range(groups):
            hit = place + g * BLOCK == jnp.broadcast_to(vir_i[pl.ds(r, 1), :], (BLOCK, BLOCK))
            ev_row[pl.ds(r, 1), :] += jnp.sum(jnp.where(hit, table, 0.0), axis=0, keepdims=True)
        return carry

    lax.fori_loop(0, groups, group, 0)
    mine = ev_row[pl.ds((x % 2) * 4 + core * 2 + x // 2, 1), :]
    ev_col[...] = jnp.transpose(jnp.broadcast_to(mine, (BLOCK, BLOCK)))


def per_device(aux_factors, occ_energy, vir_energy, occ_index, vir_index):
    occ_count = lax.axis_size("occ")
    _, width, aux_width = aux_factors.shape
    groups = vir_energy.shape[0] // BLOCK
    dma = pltpu.SemaphoreType.DMA
    in_hbm = functools.partial(pltpu.with_memory_space_constraint, memory_space=pltpu.HBM)
    result = pl.pallas_call(
        functools.partial(kernel, occ_count),
        out_shape=jax.ShapeDtypeStruct((width, aux_width), jnp.float32),
        in_specs=[pl.BlockSpec(memory_space=pltpu.HBM)] * 5,
        out_specs=pl.BlockSpec(memory_space=pltpu.VMEM),
        scratch_shapes=[
            pltpu.VMEM((STEPS, RING, 2 * BLOCK, aux_width), jnp.bfloat16),
            pltpu.VMEM((len(RELAYED), PIECE, aux_width), jnp.bfloat16),
            pltpu.VMEM((groups, BLOCK), jnp.float32),
            pltpu.VMEM((groups, BLOCK), jnp.int32),
            pltpu.VMEM((1, occ_count), jnp.float32),
            pltpu.VMEM((1, occ_count), jnp.int32),
            pltpu.VMEM((groups, BLOCK), jnp.float32),
            pltpu.VMEM((BLOCK, BLOCK), jnp.float32),
            pltpu.VMEM((8, BLOCK), jnp.float32),
            pltpu.VMEM((BLOCK, 2 * BLOCK), jnp.bfloat16),
            pltpu.VMEM((3 * BLOCK, aux_width), jnp.bfloat16),
            pltpu.VMEM((2, RING, BLOCK, 2 * BLOCK), jnp.float32),
            dma((STEPS, RING, PIECES)),
            dma((STEPS, RING, PIECES)),
            dma((len(RELAYED),)),
            dma((len(RELAYED),)),
            dma((STEPS, RING, 2)),
            dma((STEPS, RING, 2)),
            dma((6,)),
            dma((3,)),
        ],
        compiler_params=pltpu.CompilerParams(
            collective_id=0, has_side_effects=True, vmem_limit_bytes=40 << 20),
        cost_estimate=pl.CostEstimate(
            flops=6 * STEPS * width * 8 * BLOCK * aux_width, bytes_accessed=2 << 20, transcendentals=0),
    )(
        in_hbm(aux_factors.reshape(width, aux_width)),
        in_hbm(vir_energy.reshape(groups, BLOCK)),
        in_hbm(vir_index.reshape(groups, BLOCK)),
        in_hbm(occ_energy.reshape(1, occ_count)),
        in_hbm(occ_index.reshape(1, occ_count)),
    )
    return result.reshape(1, width, aux_width)


def solution(mesh):
    return jax.shard_map(
        per_device,
        mesh=mesh,
        in_specs=(P("occ", ("vb", "va"), None), P(), P(), P(), P()),
        out_specs=P("occ", ("vb", "va"), None),
        check_vma=False,
    )
```

```python
import functools

import jax
import jax.numpy as jnp
from jax import lax
from jax.experimental import pallas as pl
from jax.experimental.pallas import tpu as pltpu
from jax.sharding import PartitionSpec as P

LOGICAL = pl.DeviceIdType.LOGICAL
STEPS = 4
RING = 4
BLOCK = 128
PIECES = 4
FIRST = PIECES // 2
PIECE = BLOCK // PIECES
NT = (((1,), (1,)), ((), ()))

ORDER = (
    (0, 1),
    (0, 0),
    (3, 0),
    (1, 0),
    (3, 1),
    (0, 3),
    (3, 3),
    (1, 3),
    (1, 1),
    (0, 2),
    (2, 0),
    (3, 2),
    (1, 2),
    (2, 1),
    (2, 3),
    (2, 2),
)
PLAN = (
    (("T", 0, 3, 0), ("T", 0, 1, 0), ("R", 0), ("T", 3, 0, 2), ("XF", 0, 3, 0), ("T", 0, 1, 1), ("Y", 3, 0), ("R", 1), ("R", 2), ("Y", 1, 1), ("T", 3, 0, 3), ("XF", 0, 1, 1), ("T", 1, 0, 2), ("R", 3), ("YF", 1, 0, 2), ("T", 0, 3, 1), ("Y", 3, 1), ("T", 3, 0, 0), ("T", 0, 1, 2), ("T", 0, 1, 3), ("X", 3, 2), ("T", 0, 3, 3), ("T", 0, 3, 2), ("XF", 0, 3, 2), ("T", 1, 0, 3), ("X", 3, 3), ("R", 4), ("YF", 3, 0, 3), ("T", 3, 0, 1), ("T", 0, 2, 0), ("X", 1, 3), ("T", 3, 3, 0), ("T", 1, 0, 0), ("R", 7), ("Y", 1, 0), ("T", 3, 3, 2), ("X", 1, 2), ("Y", 2, 0), ("T", 3, 1, 2), ("T", 1, 3, 0), ("T", 1, 0, 1), ("R", 5), ("T", 3, 1, 1), ("XF", 0, 1, 3), ("R", 6), ("XF", 3, 3, 2), ("T", 0, 2, 1), ("T", 0, 2, 2), ("Y", 2, 1), ("T", 3, 1, 3), ("T", 1, 1, 1), ("T", 3, 3, 3), ("T", 1, 1, 3), ("T", 3, 3, 1)),
    (("XF", 3, 1, 3), ("T", 1, 1, 2), ("YF", 1, 0, 0), ("T", 2, 0, 3), ("T", 2, 0, 2)),
    (("X", 2, 2), ("T", 3, 1, 0), ("YF", 3, 0, 1), ("R", 8)),
    (("T", 1, 3, 2), ("X", 2, 3), ("T", 0, 2, 3)),
    (("YF", 3, 1, 1), ("T", 1, 3, 1), ("R", 9), ("XF", 1, 1, 3), ("T", 1, 1, 0), ("T", 3, 2, 0), ("YF", 1, 1, 0), ("YF", 1, 3, 0), ("T", 3, 2, 3), ("T", 1, 3, 3), ("YF", 3, 3, 1), ("XF", 1, 3, 2)),
    (("T", 3, 2, 1), ("T", 3, 2, 2)),
    (("T", 1, 2, 0), ("T", 2, 1, 2), ("YF", 1, 2, 0), ("T", 2, 3, 2), ("XF", 2, 3, 2), ("YF", 3, 2, 1), ("T", 2, 0, 0), ("T", 2, 0, 1)),
    (),
    (("T", 2, 1, 3), ("T", 1, 2, 1), ("XF", 2, 1, 3), ("T", 2, 1, 0)),
    (),
    (("T", 2, 1, 1), ("T", 1, 2, 3), ("T", 1, 2, 2), ("T", 2, 3, 3)),
    (("T", 2, 3, 0), ("T", 2, 3, 1)),
    (("T", 2, 2, 1), ("T", 2, 2, 2), ("T", 2, 2, 3), ("T", 2, 2, 0)),
    (),
    (),
    (),
)
RELAYED = (
    tuple((0, q) for q in range(FIRST, PIECES))
    + tuple((0, q) for q in range(FIRST))
    + tuple((xr, q) for xr in (3, 1, 2) for q in range(FIRST))
)


def pick(step, values):
    out = jnp.int32(values[0])
    for k, value in enumerate(values):
        if k and value != values[0]:
            out = jnp.where(step == k, jnp.int32(value), out)
    return out


def kernel(occ_count, aux, vir_e_in, vir_i_in, occ_e_in, occ_i_in, out, held, relay, vir_e, vir_i, occ_e, occ_i,
           ev_row, ev_col, eo, weights, mine, swaps, send, recv, relay_send, relay_recv, pair_send, pair_recv, own_sem, mine_sem):
    occ = lax.axis_index("occ")
    va = lax.axis_index("va")
    vb = lax.axis_index("vb")
    x = va * 2 + vb // 2
    core = vb % 2
    y = occ % RING

    va_count = lax.axis_size("va")
    vb_count = lax.axis_size("vb")

    def device(occ_shift, x_shift=0, other_core=False):
        xs = (x + x_shift + RING) % RING
        cs = 1 - core if other_core else core
        far = (occ + occ_shift + occ_count) % occ_count
        return (far * va_count + xs // 2) * vb_count + (xs % 2) * 2 + cs

    right, left_side = device(0, 1), device(0, -1)
    ahead = {k: device(k) for k in (1, -1, 3, -3, 4, -4)}
    partner = device(0, 0, True)
    first_row = y == 0
    last_row = y == RING - 1

    tables = [
        pltpu.make_async_copy(src, dst, own_sem.at[1 + k])
        for k, (src, dst) in enumerate(((vir_e_in, vir_e), (vir_i_in, vir_i), (occ_e_in, occ_e), (occ_i_in, occ_i)))
    ]
    own_copy = pltpu.make_async_copy(aux, held.at[0, 0, pl.ds(0, BLOCK)], own_sem.at[0])
    first_mine = pltpu.make_async_copy(aux, mine.at[pl.ds(0, BLOCK)], own_sem.at[5])
    peers = [*ahead.values(), right, left_side, partner]
    barrier = pltpu.get_barrier_semaphore()
    for peer in peers:
        pl.semaphore_signal(barrier, inc=1, device_id=peer, device_id_type=LOGICAL)
    own_copy.start()
    first_mine.start()
    for table in tables:
        table.start()
    pl.semaphore_wait(barrier, len(peers))

    def rows(d, xr, q):
        return held.at[d, xr, pl.ds(q * PIECE, PIECE)]

    def source(d, xr, q):
        return aux.at[pl.ds(q * PIECE, PIECE)] if d == 0 and xr == 0 else rows(d, xr, q)

    def link(src, d, xr, q, peer):
        return pltpu.make_async_remote_copy(
            src_ref=src, dst_ref=rows(d, xr, q), send_sem=send.at[d, xr, q], recv_sem=recv.at[d, xr, q],
            device_id=peer, device_id_type=LOGICAL)

    def relay_in(k, src):
        xr, q = RELAYED[k]
        return pltpu.make_async_remote_copy(
            src_ref=src, dst_ref=relay.at[k], send_sem=send.at[1, xr, q], recv_sem=relay_recv.at[k],
            device_id=ahead[-3], device_id_type=LOGICAL)

    def relay_out(k):
        xr, q = RELAYED[k]
        return pltpu.make_async_remote_copy(
            src_ref=relay.at[k], dst_ref=rows(1, xr, q), send_sem=relay_send.at[k], recv_sem=recv.at[1, xr, q],
            device_id=ahead[4], device_id_type=LOGICAL)

    def send_x(d, q):
        link(source(d, 0, q), d, 3, q, right).start()
        link(source(d, 0, q), d, 1, q, left_side).start()

    def send_y(xr, q):
        src = source(0, xr, q)

        @pl.when(last_row)
        def _():
            relay_in(RELAYED.index((xr, q)), src).start()

        @pl.when(jnp.logical_not(last_row))
        def _():
            link(src, 1, xr, q, ahead[1]).start()

        link(src, 3, xr, q, ahead[3]).start()

    def pass_relay(k):
        @pl.when(first_row)
        def _():
            relay_in(k, relay.at[k]).wait_recv()
            relay_out(k).start()

    def x_far(d, xr, q):
        if xr == 3 and q % 2 == 0:
            link(rows(d, xr, q), d, 2, q, right).start()
        if xr == 1 and q % 2 == 1:
            link(rows(d, xr, q), d, 2, q, left_side).start()

    def y_far(d, xr, q):
        if d == 1 and q % 2 == 0:
            link(rows(d, xr, q), 2, xr, q, ahead[1]).start()
        if d == 3 and q % 2 == 1:
            link(rows(d, xr, q), 2, xr, q, ahead[-1]).start()

    def pair(d, xr, h):
        span = pl.ds(h * FIRST * PIECE, FIRST * PIECE)
        src = aux.at[span] if d == 0 and xr == 0 else held.at[d, xr, span]
        return pltpu.make_async_remote_copy(
            src_ref=src, dst_ref=held.at[d, xr, pl.ds(BLOCK + h * FIRST * PIECE, FIRST * PIECE)],
            send_sem=pair_send.at[d, xr, h], recv_sem=pair_recv.at[d, xr, h],
            device_id=partner, device_id_type=LOGICAL)

    missing = {(d, xr, h): FIRST for d in range(STEPS) for xr in range(RING) for h in range(2)}

    def take(d, xr, q):
        link(rows(d, xr, q), d, xr, q, ahead[1]).wait_recv()
        h = q // FIRST
        missing[d, xr, h] -= 1
        if missing[d, xr, h] == 0:
            pair(d, xr, h).start()
            if d % 2 and xr == 0 and missing[d, 0, 1 - h] == 0:
                mine_copy(1 + d // 2).start()

    def mine_copy(k):
        return pltpu.make_async_copy(
            held.at[(0, 1, 3)[k], 0, pl.ds(0, BLOCK)], mine.at[pl.ds(k * BLOCK, BLOCK)], mine_sem.at[k])

    waited = []

    def pair_ready(d, xr):
        for h in range(2):
            pair(d, xr, h).wait_recv()
        if not waited:
            waited.append(True)
            mine_copy(1).wait()
            mine_copy(2).wait()

    actions = {"T": take, "R": pass_relay, "X": send_x, "Y": send_y, "XF": x_far, "YF": y_far}

    def events(k):
        for what, *item in PLAN[k]:
            actions[what](*item)
        pair_ready(*ORDER[k])
        if k == [o[0] for o in ORDER].index(2):
            lax.fori_loop(0, RING, swap_at_two, 0)

    for q in range(FIRST):
        send_y(0, FIRST + q)
        send_x(0, q)
    for q in range(FIRST):
        send_y(0, q)
        send_x(0, FIRST + q)
    pair(0, 0, 0).start()
    pair(0, 0, 1).start()

    out[...] = jnp.zeros_like(out)
    for table in tables:
        table.wait()
    lookup_energies(occ, occ_count, x, core, vir_e, vir_i, occ_e, occ_i, ev_row, ev_col, eo)
    own_copy.wait()
    first_mine.wait()

    def tile_of(step):
        if isinstance(step, int):
            return ORDER[step]
        return pick(step, [o[0] for o in ORDER]), pick(step, [o[1] for o in ORDER])

    def add_gradient(step):
        d, xr = tile_of(step)
        held_weights = weights[...]
        for c in range(4):
            cols = pl.ds(c * 512, 512)
            out[:, cols] += jnp.dot(held_weights, held[d, xr, :, cols], preferred_element_type=jnp.float32)

    def gap_of(d, xr):
        xs = (x + xr) % RING
        near = ev_row[pl.ds((xs % 2) * 4 + core * 2 + xs // 2, 1), :]
        far = ev_row[pl.ds((xs % 2) * 4 + (1 - core) * 2 + xs // 2, 1), :]
        base = eo[pl.ds(0, 1), :] + eo[pl.ds(d, 1), :]
        left = jnp.broadcast_to(base, (BLOCK, BLOCK)) - ev_col[...]
        return jnp.concatenate([left - near, left - far], axis=1)

    def product(left, d, xr):
        return lax.dot_general(left, held[d, xr], NT, preferred_element_type=jnp.float32)

    def swap_at_two(xr, carry):
        swaps[2, xr] = product(held[2, 0, 0:BLOCK], 0, xr)
        return carry

    def tile(step, carry):
        for k in range(len(ORDER)):
            pl.when(step == k)(functools.partial(events, k))
        before = step - jnp.minimum(step, 1)
        d, xr = tile_of(step)

        @pl.when(d == 0)
        def _():
            add_gradient(before)
            coul = product(mine[...], 0, xr)
            swaps[0, xr] = coul[BLOCK:2 * BLOCK]
            swaps[1, xr] = coul[2 * BLOCK:]
            coul = coul[:BLOCK]
            weights[...] = ((2.0 * coul - coul) / gap_of(0, xr)).astype(jnp.bfloat16)

        @pl.when(d != 0)
        def _():
            add_gradient(before)
            coul = product(mine[0:BLOCK], d, xr)
            swap = swaps[jnp.where(d == 2, 2, d // 2), xr]
            weights[...] = ((2.0 * coul - swap) / gap_of(d, xr)).astype(jnp.bfloat16)

        return carry

    weights[...] = jnp.zeros_like(weights)
    lax.fori_loop(0, len(ORDER), tile, 0)
    add_gradient(len(ORDER) - 1)

    for d in range(STEPS):
        for xr in range(RING):
            for h in range(2):
                pair(d, xr, h).wait_send()
            if d or xr:
                for q in range(PIECES):
                    link(rows(d, xr, q), d, xr, q, ahead[1]).wait_send()

    @pl.when(first_row)
    def _():
        for k in range(len(RELAYED)):
            relay_out(k).wait_send()


def lookup_energies(occ, occ_count, x, core, vir_e, vir_i, occ_e, occ_i, ev_row, ev_col, eo):
    groups = vir_e.shape[0]
    lanes = lax.broadcasted_iota(jnp.int32, occ_e.shape, 1)
    for d in range(STEPS):
        mine = lanes == (occ - d + occ_count) % occ_count
        index = jnp.sum(jnp.where(mine, occ_i[...], 0), axis=1, keepdims=True)
        value = jnp.sum(jnp.where(lanes == index, occ_e[...], 0.0), axis=1, keepdims=True)
        eo[pl.ds(d, 1), :] = jnp.broadcast_to(value, (1, BLOCK))
    ev_row[...] = jnp.zeros_like(ev_row)
    place = lax.broadcasted_iota(jnp.int32, (BLOCK, BLOCK), 0)

    def group(g, carry):
        table = jnp.transpose(jnp.broadcast_to(vir_e[pl.ds(g, 1), :], (BLOCK, BLOCK)))
        for r in range(groups):
            hit = place + g * BLOCK == jnp.broadcast_to(vir_i[pl.ds(r, 1), :], (BLOCK, BLOCK))
            ev_row[pl.ds(r, 1), :] += jnp.sum(jnp.where(hit, table, 0.0), axis=0, keepdims=True)
        return carry

    lax.fori_loop(0, groups, group, 0)
    mine = ev_row[pl.ds((x % 2) * 4 + core * 2 + x // 2, 1), :]
    ev_col[...] = jnp.transpose(jnp.broadcast_to(mine, (BLOCK, BLOCK)))


def per_device(aux_factors, occ_energy, vir_energy, occ_index, vir_index):
    occ_count = lax.axis_size("occ")
    _, width, aux_width = aux_factors.shape
    groups = vir_energy.shape[0] // BLOCK
    dma = pltpu.SemaphoreType.DMA
    in_hbm = functools.partial(pltpu.with_memory_space_constraint, memory_space=pltpu.HBM)
    result = pl.pallas_call(
        functools.partial(kernel, occ_count),
        out_shape=jax.ShapeDtypeStruct((width, aux_width), jnp.float32),
        in_specs=[pl.BlockSpec(memory_space=pltpu.HBM)] * 5,
        out_specs=pl.BlockSpec(memory_space=pltpu.VMEM),
        scratch_shapes=[
            pltpu.VMEM((STEPS, RING, 2 * BLOCK, aux_width), jnp.bfloat16),
            pltpu.VMEM((len(RELAYED), PIECE, aux_width), jnp.bfloat16),
            pltpu.VMEM((groups, BLOCK), jnp.float32),
            pltpu.VMEM((groups, BLOCK), jnp.int32),
            pltpu.VMEM((1, occ_count), jnp.float32),
            pltpu.VMEM((1, occ_count), jnp.int32),
            pltpu.VMEM((groups, BLOCK), jnp.float32),
            pltpu.VMEM((BLOCK, BLOCK), jnp.float32),
            pltpu.VMEM((8, BLOCK), jnp.float32),
            pltpu.VMEM((BLOCK, 2 * BLOCK), jnp.bfloat16),
            pltpu.VMEM((3 * BLOCK, aux_width), jnp.bfloat16),
            pltpu.VMEM((3, RING, BLOCK, 2 * BLOCK), jnp.float32),
            dma((STEPS, RING, PIECES)),
            dma((STEPS, RING, PIECES)),
            dma((len(RELAYED),)),
            dma((len(RELAYED),)),
            dma((STEPS, RING, 2)),
            dma((STEPS, RING, 2)),
            dma((6,)),
            dma((3,)),
        ],
        compiler_params=pltpu.CompilerParams(
            collective_id=0, has_side_effects=True, vmem_limit_bytes=40 << 20),
        cost_estimate=pl.CostEstimate(
            flops=6 * STEPS * width * 8 * BLOCK * aux_width, bytes_accessed=2 << 20, transcendentals=0),
    )(
        in_hbm(aux_factors.reshape(width, aux_width)),
        in_hbm(vir_energy.reshape(groups, BLOCK)),
        in_hbm(vir_index.reshape(groups, BLOCK)),
        in_hbm(occ_energy.reshape(1, occ_count)),
        in_hbm(occ_index.reshape(1, occ_count)),
    )
    return result.reshape(1, width, aux_width)


def solution(mesh):
    return jax.shard_map(
        per_device,
        mesh=mesh,
        in_specs=(P("occ", ("vb", "va"), None), P(), P(), P(), P()),
        out_specs=P("occ", ("vb", "va"), None),
        check_vma=False,
    )
```

```python
import functools

import jax
import jax.numpy as jnp
from jax import lax
from jax.experimental import pallas as pl
from jax.experimental.pallas import tpu as pltpu
from jax.sharding import PartitionSpec as P

LOGICAL = pl.DeviceIdType.LOGICAL
STEPS = 4
RING = 4
BLOCK = 128
PIECES = 4
FIRST = PIECES // 2
PIECE = BLOCK // PIECES
NT = (((1,), (1,)), ((), ()))

ORDER = (
    (0, 1),
    (0, 0),
    (3, 0),
    (1, 0),
    (3, 1),
    (0, 3),
    (3, 3),
    (1, 3),
    (1, 1),
    (0, 2),
    (2, 0),
    (3, 2),
    (1, 2),
    (2, 1),
    (2, 3),
    (2, 2),
)
PLAN = (
    (("T", 0, 3, 0), ("T", 0, 1, 0), ("R", 0), ("T", 3, 0, 2), ("XF", 0, 3, 0), ("T", 0, 1, 1), ("Y", 3, 0), ("R", 1), ("R", 2), ("Y", 1, 1), ("T", 3, 0, 3), ("XF", 0, 1, 1), ("T", 1, 0, 2), ("R", 3), ("YF", 1, 0, 2), ("T", 0, 3, 1), ("Y", 3, 1), ("T", 3, 0, 0), ("T", 0, 1, 2), ("T", 0, 1, 3), ("X", 3, 2), ("T", 0, 3, 3), ("T", 0, 3, 2), ("XF", 0, 3, 2), ("T", 1, 0, 3), ("X", 3, 3), ("R", 4), ("YF", 3, 0, 3), ("T", 3, 0, 1), ("T", 0, 2, 0), ("X", 1, 3), ("T", 3, 3, 0), ("T", 1, 0, 0), ("R", 7), ("Y", 1, 0), ("T", 3, 3, 2), ("X", 1, 2), ("Y", 2, 0), ("T", 3, 1, 2), ("T", 1, 3, 0), ("T", 1, 0, 1), ("R", 5), ("T", 3, 1, 1), ("XF", 0, 1, 3), ("R", 6), ("XF", 3, 3, 2), ("T", 0, 2, 1), ("T", 0, 2, 2), ("Y", 2, 1), ("T", 3, 1, 3), ("T", 1, 1, 1), ("T", 3, 3, 3), ("T", 1, 1, 3), ("T", 3, 3, 1)),
    (("XF", 3, 1, 3), ("T", 1, 1, 2), ("YF", 1, 0, 0), ("T", 2, 0, 3), ("T", 2, 0, 2)),
    (("X", 2, 2), ("T", 3, 1, 0), ("YF", 3, 0, 1), ("R", 8)),
    (("T", 1, 3, 2), ("X", 2, 3), ("T", 0, 2, 3)),
    (("YF", 3, 1, 1), ("T", 1, 3, 1), ("R", 9), ("XF", 1, 1, 3), ("T", 1, 1, 0), ("T", 3, 2, 0), ("YF", 1, 1, 0), ("YF", 1, 3, 0), ("T", 3, 2, 3), ("T", 1, 3, 3), ("YF", 3, 3, 1), ("XF", 1, 3, 2)),
    (("T", 3, 2, 1), ("T", 3, 2, 2)),
    (("T", 1, 2, 0), ("T", 2, 1, 2), ("YF", 1, 2, 0), ("T", 2, 3, 2), ("XF", 2, 3, 2), ("YF", 3, 2, 1), ("T", 2, 0, 0), ("T", 2, 0, 1)),
    (),
    (("T", 2, 1, 3), ("T", 1, 2, 1), ("XF", 2, 1, 3), ("T", 2, 1, 0)),
    (),
    (("T", 2, 1, 1), ("T", 1, 2, 3), ("T", 1, 2, 2), ("T", 2, 3, 3)),
    (("T", 2, 3, 0), ("T", 2, 3, 1)),
    (("T", 2, 2, 1), ("T", 2, 2, 2), ("T", 2, 2, 3), ("T", 2, 2, 0)),
    (),
    (),
    (),
)
RELAYED = (
    tuple((0, q) for q in range(FIRST, PIECES))
    + tuple((0, q) for q in range(FIRST))
    + tuple((xr, q) for xr in (3, 1, 2) for q in range(FIRST))
)


def pick(step, values):
    out = jnp.int32(values[0])
    for k, value in enumerate(values):
        if k and value != values[0]:
            out = jnp.where(step == k, jnp.int32(value), out)
    return out


def kernel(occ_count, aux, vir_e_in, vir_i_in, occ_e_in, occ_i_in, out, held, relay, vir_e, vir_i, occ_e, occ_i,
           ev_row, ev_col, eo, weights, mine, swaps, send, recv, relay_send, relay_recv, pair_send, pair_recv, own_sem, mine_sem):
    occ = lax.axis_index("occ")
    va = lax.axis_index("va")
    vb = lax.axis_index("vb")
    x = va * 2 + vb // 2
    core = vb % 2
    y = occ % RING

    va_count = lax.axis_size("va")
    vb_count = lax.axis_size("vb")

    def device(occ_shift, x_shift=0, other_core=False):
        xs = (x + x_shift + RING) % RING
        cs = 1 - core if other_core else core
        far = (occ + occ_shift + occ_count) % occ_count
        return (far * va_count + xs // 2) * vb_count + (xs % 2) * 2 + cs

    right, left_side = device(0, 1), device(0, -1)
    ahead = {k: device(k) for k in (1, -1, 3, -3, 4, -4)}
    partner = device(0, 0, True)
    first_row = y == 0
    last_row = y == RING - 1

    tables = [
        pltpu.make_async_copy(src, dst, own_sem.at[1 + k])
        for k, (src, dst) in enumerate(((vir_e_in, vir_e), (vir_i_in, vir_i), (occ_e_in, occ_e), (occ_i_in, occ_i)))
    ]
    own_copy = pltpu.make_async_copy(aux, held.at[0, 0, pl.ds(0, BLOCK)], own_sem.at[0])
    first_mine = pltpu.make_async_copy(aux, mine.at[pl.ds(0, BLOCK)], own_sem.at[5])
    peers = [*ahead.values(), right, left_side, partner]
    barrier = pltpu.get_barrier_semaphore()
    for peer in peers:
        pl.semaphore_signal(barrier, inc=1, device_id=peer, device_id_type=LOGICAL)
    own_copy.start()
    first_mine.start()
    for table in tables:
        table.start()
    pl.semaphore_wait(barrier, len(peers))

    def rows(d, xr, q):
        return held.at[d, xr, pl.ds(q * PIECE, PIECE)]

    def source(d, xr, q):
        return aux.at[pl.ds(q * PIECE, PIECE)] if d == 0 and xr == 0 else rows(d, xr, q)

    def link(src, d, xr, q, peer):
        return pltpu.make_async_remote_copy(
            src_ref=src, dst_ref=rows(d, xr, q), send_sem=send.at[d, xr, q], recv_sem=recv.at[d, xr, q],
            device_id=peer, device_id_type=LOGICAL)

    def relay_in(k, src):
        xr, q = RELAYED[k]
        return pltpu.make_async_remote_copy(
            src_ref=src, dst_ref=relay.at[k], send_sem=send.at[1, xr, q], recv_sem=relay_recv.at[k],
            device_id=ahead[-3], device_id_type=LOGICAL)

    def relay_out(k):
        xr, q = RELAYED[k]
        return pltpu.make_async_remote_copy(
            src_ref=relay.at[k], dst_ref=rows(1, xr, q), send_sem=relay_send.at[k], recv_sem=recv.at[1, xr, q],
            device_id=ahead[4], device_id_type=LOGICAL)

    def send_x(d, q):
        link(source(d, 0, q), d, 3, q, right).start()
        link(source(d, 0, q), d, 1, q, left_side).start()

    def send_y(xr, q):
        src = source(0, xr, q)

        @pl.when(last_row)
        def _():
            relay_in(RELAYED.index((xr, q)), src).start()

        @pl.when(jnp.logical_not(last_row))
        def _():
            link(src, 1, xr, q, ahead[1]).start()

        link(src, 3, xr, q, ahead[3]).start()

    def pass_relay(k):
        @pl.when(first_row)
        def _():
            relay_in(k, relay.at[k]).wait_recv()
            relay_out(k).start()

    def x_far(d, xr, q):
        if xr == 3 and q % 2 == 0:
            link(rows(d, xr, q), d, 2, q, right).start()
        if xr == 1 and q % 2 == 1:
            link(rows(d, xr, q), d, 2, q, left_side).start()

    def y_far(d, xr, q):
        if d == 1 and q % 2 == 0:
            link(rows(d, xr, q), 2, xr, q, ahead[1]).start()
        if d == 3 and q % 2 == 1:
            link(rows(d, xr, q), 2, xr, q, ahead[-1]).start()

    def pair(d, xr, h):
        span = pl.ds(h * FIRST * PIECE, FIRST * PIECE)
        src = aux.at[span] if d == 0 and xr == 0 else held.at[d, xr, span]
        return pltpu.make_async_remote_copy(
            src_ref=src, dst_ref=held.at[d, xr, pl.ds(BLOCK + h * FIRST * PIECE, FIRST * PIECE)],
            send_sem=pair_send.at[d, xr, h], recv_sem=pair_recv.at[d, xr, h],
            device_id=partner, device_id_type=LOGICAL)

    missing = {(d, xr, h): FIRST for d in range(STEPS) for xr in range(RING) for h in range(2)}

    def take(d, xr, q):
        link(rows(d, xr, q), d, xr, q, ahead[1]).wait_recv()
        h = q // FIRST
        missing[d, xr, h] -= 1
        if missing[d, xr, h] == 0:
            pair(d, xr, h).start()
            if d % 2 and xr == 0 and missing[d, 0, 1 - h] == 0:
                mine_copy(1 + d // 2).start()

    def mine_copy(k):
        return pltpu.make_async_copy(
            held.at[(0, 1, 3)[k], 0, pl.ds(0, BLOCK)], mine.at[pl.ds(k * BLOCK, BLOCK)], mine_sem.at[k])

    waited = []

    def pair_ready(d, xr):
        for h in range(2):
            pair(d, xr, h).wait_recv()
        if not waited:
            waited.append(True)
            mine_copy(1).wait()
            mine_copy(2).wait()

    actions = {"T": take, "R": pass_relay, "X": send_x, "Y": send_y, "XF": x_far, "YF": y_far}

    def events(k):
        for what, *item in PLAN[k]:
            actions[what](*item)
        pair_ready(*ORDER[k])

    for q in range(FIRST):
        send_y(0, FIRST + q)
        send_x(0, q)
    for q in range(FIRST):
        send_y(0, q)
        send_x(0, FIRST + q)
    pair(0, 0, 0).start()
    pair(0, 0, 1).start()

    out[...] = jnp.zeros_like(out)
    for table in tables:
        table.wait()
    lookup_energies(occ, occ_count, x, core, vir_e, vir_i, occ_e, occ_i, ev_row, ev_col, eo)
    own_copy.wait()
    first_mine.wait()

    def tile_of(step):
        if isinstance(step, int):
            return ORDER[step]
        return pick(step, [o[0] for o in ORDER]), pick(step, [o[1] for o in ORDER])

    def add_gradient(step):
        d, xr = tile_of(step)
        held_weights = weights[...]
        for c in range(4):
            cols = pl.ds(c * 512, 512)
            out[:, cols] += jnp.dot(held_weights, held[d, xr, :, cols], preferred_element_type=jnp.float32)

    def gap_of(d, xr):
        xs = (x + xr) % RING
        near = ev_row[pl.ds((xs % 2) * 4 + core * 2 + xs // 2, 1), :]
        far = ev_row[pl.ds((xs % 2) * 4 + (1 - core) * 2 + xs // 2, 1), :]
        base = eo[pl.ds(0, 1), :] + eo[pl.ds(d, 1), :]
        left = jnp.broadcast_to(base, (BLOCK, BLOCK)) - ev_col[...]
        return jnp.concatenate([left - near, left - far], axis=1)

    def product(left, d, xr):
        return lax.dot_general(left, held[d, xr], NT, preferred_element_type=jnp.float32)

    def tile(step, carry):
        for k in range(len(ORDER)):
            pl.when(step == k)(functools.partial(events, k))
        before = step - jnp.minimum(step, 1)
        d, xr = tile_of(step)

        @pl.when(d == 0)
        def _():
            add_gradient(before)
            coul = product(mine[...], 0, xr)
            swaps[0, xr] = coul[BLOCK:2 * BLOCK]
            swaps[1, xr] = coul[2 * BLOCK:]
            coul = coul[:BLOCK]
            weights[...] = ((2.0 * coul - coul) / gap_of(0, xr)).astype(jnp.bfloat16)

        @pl.when(d % 2 == 1)
        def _():
            add_gradient(before)
            coul = product(mine[0:BLOCK], d, xr)
            weights[...] = ((2.0 * coul - swaps[d // 2, xr]) / gap_of(d, xr)).astype(jnp.bfloat16)

        @pl.when(d == 2)
        def _():
            add_gradient(before)
            coul = product(mine[0:BLOCK], d, xr)
            swap = product(held[2, 0, 0:BLOCK], 0, xr)
            weights[...] = ((2.0 * coul - swap) / gap_of(d, xr)).astype(jnp.bfloat16)

        return carry

    weights[...] = jnp.zeros_like(weights)
    lax.fori_loop(0, len(ORDER), tile, 0)
    add_gradient(len(ORDER) - 1)

    for d in range(STEPS):
        for xr in range(RING):
            for h in range(2):
                pair(d, xr, h).wait_send()
            if d or xr:
                for q in range(PIECES):
                    link(rows(d, xr, q), d, xr, q, ahead[1]).wait_send()

    @pl.when(first_row)
    def _():
        for k in range(len(RELAYED)):
            relay_out(k).wait_send()


def lookup_energies(occ, occ_count, x, core, vir_e, vir_i, occ_e, occ_i, ev_row, ev_col, eo):
    groups = vir_e.shape[0]
    lanes = lax.broadcasted_iota(jnp.int32, occ_e.shape, 1)
    for d in range(STEPS):
        mine = lanes == (occ - d + occ_count) % occ_count
        index = jnp.sum(jnp.where(mine, occ_i[...], 0), axis=1, keepdims=True)
        value = jnp.sum(jnp.where(lanes == index, occ_e[...], 0.0), axis=1, keepdims=True)
        eo[pl.ds(d, 1), :] = jnp.broadcast_to(value, (1, BLOCK))
    ev_row[...] = jnp.zeros_like(ev_row)
    place = lax.broadcasted_iota(jnp.int32, (BLOCK, BLOCK), 0)

    def group(g, carry):
        table = jnp.transpose(jnp.broadcast_to(vir_e[pl.ds(g, 1), :], (BLOCK, BLOCK)))
        for r in range(groups):
            hit = place + g * BLOCK == jnp.broadcast_to(vir_i[pl.ds(r, 1), :], (BLOCK, BLOCK))
            ev_row[pl.ds(r, 1), :] += jnp.sum(jnp.where(hit, table, 0.0), axis=0, keepdims=True)
        return carry

    lax.fori_loop(0, groups, group, 0)
    mine = ev_row[pl.ds((x % 2) * 4 + core * 2 + x // 2, 1), :]
    ev_col[...] = jnp.transpose(jnp.broadcast_to(mine, (BLOCK, BLOCK)))


def per_device(aux_factors, occ_energy, vir_energy, occ_index, vir_index):
    occ_count = lax.axis_size("occ")
    _, width, aux_width = aux_factors.shape
    groups = vir_energy.shape[0] // BLOCK
    dma = pltpu.SemaphoreType.DMA
    in_hbm = functools.partial(pltpu.with_memory_space_constraint, memory_space=pltpu.HBM)
    result = pl.pallas_call(
        functools.partial(kernel, occ_count),
        out_shape=jax.ShapeDtypeStruct((width, aux_width), jnp.float32),
        in_specs=[pl.BlockSpec(memory_space=pltpu.HBM)] * 5,
        out_specs=pl.BlockSpec(memory_space=pltpu.VMEM),
        scratch_shapes=[
            pltpu.VMEM((STEPS, RING, 2 * BLOCK, aux_width), jnp.bfloat16),
            pltpu.VMEM((len(RELAYED), PIECE, aux_width), jnp.bfloat16),
            pltpu.VMEM((groups, BLOCK), jnp.float32),
            pltpu.VMEM((groups, BLOCK), jnp.int32),
            pltpu.VMEM((1, occ_count), jnp.float32),
            pltpu.VMEM((1, occ_count), jnp.int32),
            pltpu.VMEM((groups, BLOCK), jnp.float32),
            pltpu.VMEM((BLOCK, BLOCK), jnp.float32),
            pltpu.VMEM((8, BLOCK), jnp.float32),
            pltpu.VMEM((BLOCK, 2 * BLOCK), jnp.bfloat16),
            pltpu.VMEM((3 * BLOCK, aux_width), jnp.bfloat16),
            pltpu.VMEM((2, RING, BLOCK, 2 * BLOCK), jnp.float32),
            dma((STEPS, RING, PIECES)),
            dma((STEPS, RING, PIECES)),
            dma((len(RELAYED),)),
            dma((len(RELAYED),)),
            dma((STEPS, RING, 2)),
            dma((STEPS, RING, 2)),
            dma((6,)),
            dma((3,)),
        ],
        compiler_params=pltpu.CompilerParams(
            collective_id=0, has_side_effects=True, vmem_limit_bytes=40 << 20),
        cost_estimate=pl.CostEstimate(
            flops=6 * STEPS * width * 8 * BLOCK * aux_width, bytes_accessed=2 << 20, transcendentals=0),
    )(
        in_hbm(aux_factors.reshape(width, aux_width)),
        in_hbm(vir_energy.reshape(groups, BLOCK)),
        in_hbm(vir_index.reshape(groups, BLOCK)),
        in_hbm(occ_energy.reshape(1, occ_count)),
        in_hbm(occ_index.reshape(1, occ_count)),
    )
    return result.reshape(1, width, aux_width)


def solution(mesh):
    return jax.shard_map(
        per_device,
        mesh=mesh,
        in_specs=(P("occ", ("vb", "va"), None), P(), P(), P(), P()),
        out_specs=P("occ", ("vb", "va"), None),
        check_vma=False,
    )
```
